32 devices in a mesh: wide: 8 (over z, core), col: 4 (over y, x).
Axes of the slice: x: 2, y: 2, z: 4, core: 2. Of those that a mesh axis runs over, the one named last changes fastest.
Arguments:
- amplitudes: float32 [2048, 2048], P('wide', 'col'), may hold values from -6 to 6
- integrals: float32 [2048, 2048], P('wide', 'col'), may hold values from -0.125 to 0.125
Outputs:
- ladder: float32 [2048, 2048], P(('wide', 'col'))
The draws below stay inside these ranges and needn't reach their ends.
All inputs are finite; a program needn't handle non-finite values.
Results may differ from the reference program's by a relative error of at most 0.00007.
Values sent between devices are 32-bit elements; how exact they have to be, the bound alone decides.
A program may use at most 64 MiB of HBM per device.

```python
import jax
import jax.numpy as jnp
from jax import lax

IJ = 2048
CD = 2048
AB = 2048


def shard_levels(stream_key, dims, pieces, least, largest):
    def one(dim, parts):
        steps = jax.random.uniform(jax.random.fold_in(jax.random.fold_in(stream_key, 6), dim), (parts,), jnp.float32, least / len(pieces), largest / len(pieces))
        return jnp.repeat(jnp.exp(steps), dims[dim] // parts).reshape((-1,) + (1,) * (len(dims) - dim - 1))

    factor_of = one(*pieces[0])
    for cut in pieces[1:]:
        factor_of = factor_of * one(*cut)
    return factor_of


def scatter_about(own_key, extent, width, reach, shards=(), kind=jnp.bfloat16):
    entries = jax.random.normal(own_key, extent, jnp.float32) * width
    if len(shards) > 0:
        entries = shard_levels(own_key, extent, shards, -0.22, 0.18) * entries
    return jnp.clip(entries, min=-reach, max=reach).astype(kind)


def setup_inputs(seed: int = 0) -> dict:
    key_list = jax.random.split(jax.random.key(seed), 3)
    amplitudes = scatter_about(key_list[0], (IJ, CD), 1.0, 6.0, ((0, 8), (1, 4)), jnp.float32)
    integrals = scatter_about(key_list[1], (AB, CD), CD ** -0.5, 0.125, ((0, 8), (1, 4)), jnp.float32)
    return {"amplitudes": amplitudes, "integrals": integrals}


def reference(amplitudes, integrals):
    return lax.dot_general(amplitudes, integrals, (((1,), (1,)), ((), ())), precision=lax.Precision.HIGHEST, preferred_element_type=jnp.float32)
```

```python
import functools

import jax
import jax.numpy as jnp
from jax import lax
from jax.experimental import pallas as pl
from jax.experimental.pallas import tpu as pltpu
from jax.sharding import PartitionSpec as P

MESH = pl.DeviceIdType.MESH
CORES = 2
PIECES = 2
LENT = PIECES - 1


def halves(x):
    high = x.astype(jnp.bfloat16)
    low = (x - high.astype(jnp.float32)).astype(jnp.bfloat16)
    return high, low


def dot(x, y):
    return lax.dot_general(x, y, (((1,), (1,)), ((), ())), preferred_element_type=jnp.float32)


def kernel(wide, cols, a_hbm, b_hbm, o_ref, a_ref, b_ref, load_sem, panel, a_high, a_low, part, landed,
           guest, guest_high, guest_low, outbox, inbox,
           send_line, send_pair, recv_panel, send_sum, recv_sum,
           send_guest, recv_guest, send_back, recv_back):
    w = lax.axis_index("wide")
    c = lax.axis_index("col")
    line = wide // CORES
    g = w // CORES
    core = w % CORES
    sibling = g * CORES + 1 - core
    rows = b_ref.shape[0] // PIECES
    share = o_ref.shape[0]
    slots = wide * PIECES
    extra = CORES
    far = line - 2
    left_end, right_end = g == 0, g == line - 1
    helps_left, helps_right = g == 1, g == far
    is_end = left_end | right_end
    helps = helps_left | helps_right
    partner = jnp.where(left_end | helps_right, w + CORES, w - CORES)
    chip_slots = CORES * PIECES
    missing = jnp.where(left_end, slots - chip_slots, 0) + LENT

    def kept(slot):
        lacks = (left_end & (slot >= slots - chip_slots)) | (right_end & (slot < chip_slots))
        return ~(lacks & (slot % PIECES == LENT))

    load_a = pltpu.make_async_copy(a_hbm, a_ref, load_sem.at[0])
    load_b = pltpu.make_async_copy(b_hbm, b_ref, load_sem.at[1])
    load_b.start()
    load_a.start()
    barrier = pltpu.get_barrier_semaphore()

    def greet(wide_index, col_index):
        pl.semaphore_signal(barrier, inc=1, device_id={"wide": wide_index, "col": col_index}, device_id_type=MESH)

    has_left = g > 0
    has_right = g < line - 1
    pl.when(has_left)(lambda: greet(w - CORES, c))
    pl.when(has_right)(lambda: greet(w + CORES, c))
    greet(sibling, c)

    @pl.loop(1, cols)
    def _(j):
        greet(w, (c + j) % cols)

    pl.semaphore_wait(barrier, cols + has_left.astype(jnp.int32) + has_right.astype(jnp.int32))

    load_b.wait()

    def push(src, slot, sem, target):
        return pltpu.make_async_remote_copy(
            src_ref=src, dst_ref=panel.at[slot], send_sem=sem, recv_sem=recv_panel.at[slot],
            device_id={"wide": target, "col": c}, device_id_type=MESH)

    def own(h):
        return b_ref.at[pl.ds(h * rows, rows)]

    def arrive(slot):
        pltpu.make_async_copy(panel.at[slot], panel.at[slot], recv_panel.at[slot]).wait()

    def lend():
        return pltpu.make_async_remote_copy(
            src_ref=a_ref, dst_ref=guest, send_sem=send_guest, recv_sem=recv_guest,
            device_id={"wide": partner, "col": c}, device_id_type=MESH)

    def give_back(i):
        return pltpu.make_async_remote_copy(
            src_ref=outbox.at[i], dst_ref=inbox.at[i], send_sem=send_back.at[i], recv_sem=recv_back.at[i],
            device_id={"wide": partner, "col": c}, device_id_type=MESH)

    def contract(block, slot):
        contract_rows(a_high, a_low, block, slot)

    def contract_guest(slot, i):
        contract_rows(guest_high, guest_low, panel[slot], slots + i)

    def contract_rows(rows_high, rows_low, block, slot):
        high, low = halves(block)
        product = dot(rows_high[...], high) + (dot(rows_high[...], low) + dot(rows_low[...], high))
        for k in range(cols):
            part[slot, k] = product[k * share:(k + 1) * share]

        @pl.loop(1, cols)
        def _(j):
            peer = (c + j) % cols
            pltpu.make_async_remote_copy(
                src_ref=part.at[slot, peer], dst_ref=landed.at[slot, cols - 1 - j],
                send_sem=send_sum.at[slot], recv_sem=recv_sum.at[slot],
                device_id={"wide": w, "col": peer}, device_id_type=MESH).start()

    for h in range(PIECES):
        slot = w * PIECES + h
        pl.when(has_right)(lambda: push(own(h), slot, send_line.at[slot], w + CORES).start())
        pl.when(has_left)(lambda: push(own(h), slot, send_line.at[wide * PIECES + h], w - CORES).start())
        push(own(h), slot, send_pair.at[slot], sibling).start()

    load_a.wait()
    high, low = halves(a_ref[...])
    a_high[...] = high
    a_low[...] = low
    for h in range(PIECES):
        contract(b_ref[h * rows:(h + 1) * rows], w * PIECES + h)
    for h in range(PIECES):
        slot = sibling * PIECES + h
        arrive(slot)
        contract(panel[slot], slot)

    @pl.loop(1, line)
    def _(d):
        @pl.loop(0, PIECES)
        def _(h):
            left_slot = (w - d * CORES) * PIECES + h
            right_slot = (w + d * CORES) * PIECES + h
            pair_left = (sibling - d * CORES) * PIECES + h
            pair_right = (sibling + d * CORES) * PIECES + h

            @pl.when((g - d >= 0) & ((d <= far) | (h < LENT)))
            def _():
                arrive(left_slot)
                pl.when(has_right & ((d < far) | ((d == far) & (h < LENT))))(lambda: push(panel.at[left_slot], left_slot, send_line.at[left_slot], w + CORES).start())
                push(panel.at[left_slot], left_slot, send_pair.at[left_slot], sibling).start()

            @pl.when((g + d < line) & ((d <= far) | (h < LENT)))
            def _():
                arrive(right_slot)
                pl.when(has_left & ((d < far) | ((d == far) & (h < LENT))))(lambda: push(panel.at[right_slot], right_slot, send_line.at[right_slot], w - CORES).start())
                push(panel.at[right_slot], right_slot, send_pair.at[right_slot], sibling).start()

            pl.when(is_end & (d == 1) & (h == PIECES - 1))(lambda: lend().start())

            @pl.when((g - d >= 0) & ((d <= far) | (h < LENT)))
            def _():
                contract(panel[left_slot], left_slot)

            @pl.when((g + d < line) & ((d <= far) | (h < LENT)))
            def _():
                contract(panel[right_slot], right_slot)

            @pl.when((g - d >= 0) & ((d <= far) | (h < LENT)))
            def _():
                arrive(pair_left)
                contract(panel[pair_left], pair_left)

            @pl.when((g + d < line) & ((d <= far) | (h < LENT)))
            def _():
                arrive(pair_right)
                contract(panel[pair_right], pair_right)

    def summed(slot):
        pltpu.make_async_copy(landed.at[slot], landed.at[slot], recv_sum.at[slot]).wait()
        total = part[slot, c]
        for k in range(cols - 1):
            total = total + landed[slot, k]
        return total

    def place(slot, block):
        o_ref[:, pl.ds(pl.multiple_of(slot * rows, rows), rows)] = block

    @pl.when(helps)
    def _():
        pltpu.make_async_copy(guest, guest, recv_guest).wait()
        high, low = halves(guest[...])
        guest_high[...] = high
        guest_low[...] = low
        start = jnp.where(helps_left, slots - chip_slots, 0) + LENT

        @pl.loop(0, extra)
        def _(i):
            contract_guest(start + i * PIECES, i)

        @pl.loop(0, extra)
        def _(i):
            outbox[i] = summed(slots + i)
            give_back(i).start()

    @pl.loop(0, slots)
    def _(slot):
        pl.when(kept(slot))(lambda: place(slot, summed(slot)))

    @pl.when(is_end)
    def _():
        @pl.loop(0, extra)
        def _(i):
            pltpu.make_async_copy(inbox.at[i], inbox.at[i], recv_back.at[i]).wait()
            place(missing + i * PIECES, inbox[i])

    for h in range(PIECES):
        slot = w * PIECES + h
        pl.when(has_right)(lambda: push(own(h), slot, send_line.at[slot], w + CORES).wait_send())
        pl.when(has_left)(lambda: push(own(h), slot, send_line.at[wide * PIECES + h], w - CORES).wait_send())
        push(own(h), slot, send_pair.at[slot], sibling).wait_send()

    @pl.loop(1, line)
    def _(d):
        @pl.loop(0, PIECES)
        def _(h):
            left_slot = (w - d * CORES) * PIECES + h
            right_slot = (w + d * CORES) * PIECES + h

            @pl.when((g - d >= 0) & ((d <= far) | (h < LENT)))
            def _():
                pl.when(has_right & ((d < far) | ((d == far) & (h < LENT))))(lambda: push(panel.at[left_slot], left_slot, send_line.at[left_slot], w + CORES).wait_send())
                push(panel.at[left_slot], left_slot, send_pair.at[left_slot], sibling).wait_send()

            @pl.when((g + d < line) & ((d <= far) | (h < LENT)))
            def _():
                pl.when(has_left & ((d < far) | ((d == far) & (h < LENT))))(lambda: push(panel.at[right_slot], right_slot, send_line.at[right_slot], w - CORES).wait_send())
                push(panel.at[right_slot], right_slot, send_pair.at[right_slot], sibling).wait_send()

    def sent(slot):
        pltpu.make_async_copy(landed.at[slot], landed.at[slot], send_sum.at[slot]).wait()

    @pl.loop(0, slots)
    def _(slot):
        pl.when(kept(slot))(lambda: sent(slot))

    @pl.when(helps)
    def _():
        @pl.loop(0, extra)
        def _(i):
            sent(slots + i)
            give_back(i).wait_send()

    pl.when(is_end)(lambda: lend().wait_send())


def on_device(wide, cols, amplitudes, integrals):
    rows_a, depth = amplitudes.shape
    rows_b = integrals.shape[0]
    share = rows_a // cols
    slots = wide * PIECES
    extra = CORES
    rows = rows_b // PIECES
    vmem = pl.BlockSpec(memory_space=pltpu.VMEM)
    padded = -(-share // 8) * 8
    held = 4 * (4 * rows_a * depth + (slots + PIECES) * rows * depth + (slots + extra) * 2 * cols * padded * rows)
    limit = held + 12 * 1024 * 1024
    return pl.pallas_call(
        functools.partial(kernel, wide, cols),
        out_shape=jax.ShapeDtypeStruct((share, wide * rows_b), jnp.float32),
        in_specs=[pl.BlockSpec(memory_space=pltpu.HBM)] * 2,
        out_specs=vmem,
        scratch_shapes=[
            pltpu.VMEM((rows_a, depth), jnp.float32),
            pltpu.VMEM((rows_b, depth), jnp.float32),
            pltpu.SemaphoreType.DMA((2,)),
            pltpu.VMEM((slots, rows, depth), jnp.float32),
            pltpu.VMEM((rows_a, depth), jnp.bfloat16),
            pltpu.VMEM((rows_a, depth), jnp.bfloat16),
            pltpu.VMEM((slots + extra, cols, share, rows), jnp.float32),
            pltpu.VMEM((slots + extra, cols - 1, share, rows), jnp.float32),
            pltpu.VMEM((rows_a, depth), jnp.float32),
            pltpu.VMEM((rows_a, depth), jnp.bfloat16),
            pltpu.VMEM((rows_a, depth), jnp.bfloat16),
            pltpu.VMEM((extra, share, rows), jnp.float32),
            pltpu.VMEM((extra, share, rows), jnp.float32),
            pltpu.SemaphoreType.DMA((slots + PIECES,)),
            pltpu.SemaphoreType.DMA((slots,)),
            pltpu.SemaphoreType.DMA((slots,)),
            pltpu.SemaphoreType.DMA((slots + extra,)),
            pltpu.SemaphoreType.DMA((slots + extra,)),
            pltpu.SemaphoreType.DMA,
            pltpu.SemaphoreType.DMA,
            pltpu.SemaphoreType.DMA((extra,)),
            pltpu.SemaphoreType.DMA((extra,)),
        ],
        compiler_params=pltpu.CompilerParams(
            collective_id=0, has_side_effects=True, vmem_limit_bytes=limit),
    )(pltpu.with_memory_space_constraint(amplitudes, pltpu.HBM), pltpu.with_memory_space_constraint(integrals, pltpu.HBM))


def solution(mesh):
    return jax.shard_map(
        functools.partial(on_device, mesh.shape["wide"], mesh.shape["col"]),
        mesh=mesh,
        in_specs=(P("wide", "col"), P("wide", "col")),
        out_specs=P(("wide", "col"), None),
        check_vma=False,
    )
```

```python
import functools

import jax
import jax.numpy as jnp
from jax import lax
from jax.experimental import pallas as pl
from jax.experimental.pallas import tpu as pltpu
from jax.sharding import PartitionSpec as P

MESH = pl.DeviceIdType.MESH
CORES = 2
PIECES = 2
CUTS = 4
LEAD = 2


def halves(x):
    high = x.astype(jnp.bfloat16)
    low = (x - high.astype(jnp.float32)).astype(jnp.bfloat16)
    return high, low


def dot(x, y):
    return lax.dot_general(x, y, (((1,), (1,)), ((), ())), preferred_element_type=jnp.float32)


def factors(cols):
    low = max(k for k in range(1, cols + 1) if cols % k == 0 and k * k <= cols)
    return low, cols // low


def kernel(wide, cols, a_hbm, b_hbm, o_ref, a_ref, guest, a_high, a_low, panel, part, near, mid, landed, outbox, inbox,
           load_a, load_b, send_right, send_left, recv_panel, send_a, recv_a, send_lend, recv_lend, send_guest, recv_guest,
           send_near, recv_near, send_sum, recv_sum, send_back, recv_back):
    w = lax.axis_index("wide")
    c = lax.axis_index("col")
    line = wide // CORES
    g = w // CORES
    core = w % CORES
    sibling = g * CORES + 1 - core
    low_size, high_size = factors(cols)
    square = low_size == high_size
    c_low, c_high = c % low_size, c // low_size
    share = o_ref.shape[0]
    rows = panel.shape[1]
    cut = rows // CUTS
    own_slot = g * PIECES
    slots = line * PIECES
    has_left, has_right = g > 0, g < line - 1
    left_end, right_end = g == 0, g == line - 1
    helps_left, helps_right = g == 1, g == line - 2
    is_end, helps = left_end | right_end, helps_left | helps_right
    partner = jnp.where(left_end | helps_right, w + CORES, w - CORES)

    def low_first(slot):
        if not square:
            return jnp.bool_(True)
        return jnp.where(slot < slots, (slot + (slot >= own_slot + PIECES)) % 2, slot % 2) == 0

    firsts = low_size
    seconds = high_size

    def place_of(slot):
        flip = low_first(slot)
        return jnp.where(flip, c_low, c_high), jnp.where(flip, c_high, c_low)

    def col_of(slot, first, second):
        return jnp.where(low_first(slot), second * low_size + first, first * low_size + second)

    def at(wide_index, col_index):
        return {"wide": wide_index, "col": col_index}

    def remote(src, dst, send, recv, target):
        return pltpu.make_async_remote_copy(
            src_ref=src, dst_ref=dst, send_sem=send, recv_sem=recv, device_id=target, device_id_type=MESH)

    def loading(h):
        return pltpu.make_async_copy(b_hbm.at[pl.ds(h * rows, rows)], panel.at[own_slot + h], load_b.at[h])

    load = pltpu.make_async_copy(a_hbm, a_ref.at[core], load_a)
    for h in range(PIECES):
        loading(h).start()
    load.start()

    barrier = pltpu.get_barrier_semaphore()

    def greet(wide_index, col_index):
        pl.semaphore_signal(barrier, inc=1, device_id=at(wide_index, col_index), device_id_type=MESH)

    pl.when(has_left)(lambda: greet(w - CORES, c))
    pl.when(has_right)(lambda: greet(w + CORES, c))
    greet(sibling, c)
    for j in range(1, low_size):
        peer = c_high * low_size + (c_low + j) % low_size
        greet(w, peer)
        if square:
            greet(sibling, peer)
    for j in range(1, high_size):
        peer = (c_high + j) % high_size * low_size + c_low
        greet(w, peer)
        greet(sibling, peer)
    met = 1 + (low_size - 1) * (2 if square else 1) + (high_size - 1) * 2
    pl.semaphore_wait(barrier, met + has_left.astype(jnp.int32) + has_right.astype(jnp.int32))

    def view(slot, v):
        return panel.at[slot, pl.ds(v * cut, cut)]

    def push_right(slot, v):
        return remote(view(slot, v), view(slot, v), send_right.at[slot, v], recv_panel.at[slot, v], at(w + CORES, c))

    def push_left(slot, v):
        return remote(view(slot, v), view(slot, v), send_left.at[slot, v], recv_panel.at[slot, v], at(w - CORES, c))

    def arrive(slot, v):
        pltpu.make_async_copy(view(slot, v), view(slot, v), recv_panel.at[slot, v]).wait()

    def share_a():
        return remote(a_ref.at[core], a_ref.at[core], send_a, recv_a, at(sibling, c))

    def lend():
        return remote(a_ref.at[core], guest.at[core], send_lend, recv_lend, at(partner, c))

    def share_guest():
        return remote(guest.at[core], guest.at[core], send_guest, recv_guest, at(sibling, c))

    def give_back(k, h):
        i = k * PIECES + h
        return remote(outbox.at[i], inbox.at[i], send_back.at[i], recv_back.at[i], at(partner, c))

    send_own_right = has_right & ~helps_right
    send_own_left = has_left & ~helps_left
    for h in range(PIECES):
        loading(h).wait()
        for v in range(CUTS):
            pl.when(send_own_right)(lambda: push_right(own_slot + h, v).start())
            pl.when(send_own_left)(lambda: push_left(own_slot + h, v).start())
            if h == 0 and v == 0:
                load.wait()
                share_a().start()
            if h == 0 and v == LEAD - 1:
                pl.when(is_end)(lambda: lend().start())

    def take_rows(i, block):
        high, low = halves(block)
        a_high[i] = high
        a_low[i] = low

    def contract(base, source, slot):
        high, low = halves(panel[source])
        rows_high = a_high[pl.ds(base, CORES)].reshape(CORES * cols * share, -1)
        rows_low = a_low[pl.ds(base, CORES)].reshape(CORES * cols * share, -1)
        product = dot(rows_high, high) + (dot(rows_high, low) + dot(rows_low, high))
        flip = low_first(slot)
        for k in range(CORES):
            for j in range(cols):
                first = jnp.where(flip, j % low_size, j // low_size)
                second = jnp.where(flip, j // low_size, j % low_size)
                start = (k * cols + j) * share
                part[slot, first, k, second] = product[start:start + share]
        first, second = place_of(slot)
        for j in range(1, firsts):
            peer = (first + j) % firsts
            remote(part.at[slot, peer], near.at[slot, firsts - 1 - j], send_near.at[slot], recv_near.at[slot],
                   at(w, col_of(slot, peer, second))).start()

    def combine(slot):
        pltpu.make_async_copy(near.at[slot], near.at[slot], recv_near.at[slot]).wait()
        first, second = place_of(slot)
        total = part[slot, first]
        for j in range(firsts - 1):
            total = total + near[slot, j]
        mid[slot] = total
        for j in range(1, seconds):
            peer = (second + j) % seconds
            remote(mid.at[slot, core, peer], landed.at[core, slot, seconds - 1 - j], send_sum.at[slot],
                   recv_sum.at[core, slot], at(w, col_of(slot, first, peer))).start()
        for j in range(seconds):
            peer = (second + j) % seconds
            remote(mid.at[slot, 1 - core, peer], landed.at[core, slot, second], send_sum.at[slot],
                   recv_sum.at[core, slot], at(sibling, col_of(slot, first, peer))).start()

    def finish(slot, put):
        _, second = place_of(slot)
        inner = landed.at[core, slot, pl.ds(0, seconds - 1)]
        pltpu.make_async_copy(inner, inner, recv_sum.at[core, slot]).wait()
        total = mid[slot, core, second]
        for j in range(seconds - 1):
            total = total + landed[core, slot, j]
        put(core, total)
        outer = landed.at[1 - core, slot]
        pltpu.make_async_copy(outer, outer, recv_sum.at[1 - core, slot]).wait()
        total = landed[1 - core, slot, 0]
        for j in range(1, seconds):
            total = total + landed[1 - core, slot, j]
        put(1 - core, total)

    def place(slot, k, block):
        start = ((slot // PIECES) * CORES + k) * PIECES + slot % PIECES
        o_ref[:, pl.ds(pl.multiple_of(start * rows, rows), rows)] = block

    take_rows(core, a_ref[core])
    pltpu.make_async_copy(a_ref.at[1 - core], a_ref.at[1 - core], recv_a).wait()
    take_rows(1 - core, a_ref[1 - core])

    def left_of(t):
        d = t // PIECES
        return (t >= 0) & (g >= d) & ~(right_end & (d == 1)), (g - d) * PIECES + t % PIECES

    def right_of(t):
        d = t // PIECES
        return (d >= 1) & (g + d < line) & ~(left_end & (d == 1)), (g + d) * PIECES + t % PIECES

    def each(t, act):
        @pl.loop(0, 2)
        def _(side):
            left, left_slot = left_of(t)
            right, right_slot = right_of(t)
            pl.when(jnp.where(side == 0, left, right))(lambda: act(jnp.where(side == 0, left_slot, right_slot)))

    guest_at = 2 * PIECES

    @pl.loop(0, slots + 1)
    def _(t):
        left, left_slot = left_of(t)
        right, right_slot = right_of(t)

        @pl.loop(0, CUTS)
        def _(v):
            @pl.when(left & (t >= PIECES))
            def _():
                arrive(left_slot, v)
                pl.when(has_right)(lambda: push_right(left_slot, v).start())

            @pl.when(right)
            def _():
                arrive(right_slot, v)
                pl.when(has_left)(lambda: push_left(right_slot, v).start())

            @pl.when(helps & (t == guest_at) & (v == 1))
            def _():
                pltpu.make_async_copy(guest.at[core], guest.at[core], recv_lend).wait()
                share_guest().start()
                take_rows(CORES + core, guest[core])

            @pl.when(helps & (t == guest_at) & (v == 2))
            def _():
                pltpu.make_async_copy(guest.at[1 - core], guest.at[1 - core], recv_guest).wait()
                take_rows(CORES + 1 - core, guest[1 - core])

                @pl.loop(0, PIECES)
                def _(h):
                    contract(CORES, own_slot + h, slots + h)

            @pl.when(v == 2)
            def _():
                each(t - 1, combine)

            @pl.when(helps & (t == guest_at + 1) & (v == 0))
            def _():
                @pl.loop(0, PIECES)
                def _(h):
                    combine(slots + h)

            @pl.when(helps & (t == guest_at + 1) & (v == 2))
            def _():
                @pl.loop(0, PIECES)
                def _(h):
                    def put(k, block):
                        outbox[k * PIECES + h] = block
                        give_back(k, h).start()

                    finish(slots + h, put)

            @pl.when(v == 1)
            def _():
                each(t - 2, lambda slot: finish(slot, functools.partial(place, slot)))

        @pl.when(t < slots)
        def _():
            each(t, lambda slot: contract(0, slot, slot))

    each(slots - 1, lambda slot: finish(slot, functools.partial(place, slot)))

    @pl.when(is_end)
    def _():
        origin = jnp.where(left_end, 1, line - 2) * PIECES

        @pl.loop(0, CORES)
        def _(k):
            @pl.loop(0, PIECES)
            def _(h):
                i = k * PIECES + h
                pltpu.make_async_copy(inbox.at[i], inbox.at[i], recv_back.at[i]).wait()
                place(origin + h, k, inbox[i])

    def settle(slot):
        out = near.at[slot]
        pltpu.make_async_copy(out, out, send_near.at[slot]).wait()
        inner = landed.at[core, slot, pl.ds(0, seconds - 1)]
        outer = landed.at[core, slot]
        pltpu.make_async_copy(inner, inner, send_sum.at[slot]).wait()
        pltpu.make_async_copy(outer, outer, send_sum.at[slot]).wait()

    @pl.loop(0, slots)
    def _(t):
        left, left_slot = left_of(t)
        right, right_slot = right_of(t)
        own = t < PIECES

        @pl.loop(0, CUTS)
        def _(v):
            pl.when(left & jnp.where(own, send_own_right, has_right))(lambda: push_right(left_slot, v).wait_send())
            pl.when(own & send_own_left)(lambda: push_left(left_slot, v).wait_send())
            pl.when(right & has_left)(lambda: push_left(right_slot, v).wait_send())

        each(t, settle)

    share_a().wait_send()

    @pl.when(helps)
    def _():
        share_guest().wait_send()

        @pl.loop(0, PIECES)
        def _(h):
            settle(slots + h)
            for k in range(CORES):
                give_back(k, h).wait_send()

    pl.when(is_end)(lambda: lend().wait_send())


def on_device(wide, cols, amplitudes, integrals):
    rows_a, depth = amplitudes.shape
    rows_b = integrals.shape[0]
    share = rows_a // cols
    line = wide // CORES
    low_size, high_size = factors(cols)
    slots = line * PIECES
    total = slots + PIECES
    rows = rows_b // PIECES
    padded = -(-share // 8) * 8
    block = padded * rows
    back = CORES * PIECES
    dma = pltpu.SemaphoreType.DMA
    held = 4 * (6 * CORES * rows_a * depth + slots * rows * depth + 2 * back * block
                + total * CORES * high_size * block * (2 * low_size + 2) + share * wide * rows_b)
    return pl.pallas_call(
        functools.partial(kernel, wide, cols),
        out_shape=jax.ShapeDtypeStruct((share, wide * rows_b), jnp.float32),
        in_specs=[pl.BlockSpec(memory_space=pltpu.HBM)] * 2,
        out_specs=pl.BlockSpec(memory_space=pltpu.VMEM),
        scratch_shapes=[
            pltpu.VMEM((CORES, rows_a, depth), jnp.float32),
            pltpu.VMEM((CORES, rows_a, depth), jnp.float32),
            pltpu.VMEM((2 * CORES, rows_a, depth), jnp.bfloat16),
            pltpu.VMEM((2 * CORES, rows_a, depth), jnp.bfloat16),
            pltpu.VMEM((slots, rows, depth), jnp.float32),
            pltpu.VMEM((total, low_size, CORES, high_size, share, rows), jnp.float32),
            pltpu.VMEM((total, low_size - 1, CORES, high_size, share, rows), jnp.float32),
            pltpu.VMEM((total, CORES, high_size, share, rows), jnp.float32),
            pltpu.VMEM((CORES, total, high_size, share, rows), jnp.float32),
            pltpu.VMEM((back, share, rows), jnp.float32),
            pltpu.VMEM((back, share, rows), jnp.float32),
            dma,
            dma((PIECES,)),
            dma((slots, CUTS)),
            dma((slots, CUTS)),
            dma((slots, CUTS)),
            dma, dma, dma, dma, dma, dma,
            dma((total,)),
            dma((total,)),
            dma((total,)),
            dma((CORES, total)),
            dma((back,)),
            dma((back,)),
        ],
        compiler_params=pltpu.CompilerParams(
            collective_id=0, has_side_effects=True, vmem_limit_bytes=held + 12 * 1024 * 1024),
    )(pltpu.with_memory_space_constraint(amplitudes, pltpu.HBM), pltpu.with_memory_space_constraint(integrals, pltpu.HBM))


def solution(mesh):
    return jax.shard_map(
        functools.partial(on_device, mesh.shape["wide"], mesh.shape["col"]),
        mesh=mesh,
        in_specs=(P("wide", "col"), P("wide", "col")),
        out_specs=P(("wide", "col"), None),
        check_vma=False,
    )
```

```python
import functools

import jax
import jax.numpy as jnp
from jax import lax
from jax.experimental import pallas as pl
from jax.experimental.pallas import tpu as pltpu
from jax.sharding import PartitionSpec as P

MESH = pl.DeviceIdType.MESH
CORES = 2
PIECES = 2
KEPT = 1


def halves(x):
    high = x.astype(jnp.bfloat16)
    low = (x - high.astype(jnp.float32)).astype(jnp.bfloat16)
    return high, low


def dot(x, y):
    return lax.dot_general(x, y, (((1,), (1,)), ((), ())), preferred_element_type=jnp.float32)


def kernel(wide, cols, a_hbm, b_hbm, o_ref, a_ref, b_ref, load_sem, panel, a_high, a_low, part, landed,
           guest, guest_high, guest_low, outbox, inbox,
           send_line, send_pair, recv_panel, send_sum, recv_sum,
           send_guest, recv_guest, send_back, recv_back):
    w = lax.axis_index("wide")
    c = lax.axis_index("col")
    line = wide // CORES
    g = w // CORES
    core = w % CORES
    sibling = g * CORES + 1 - core
    rows = b_ref.shape[0] // PIECES
    share = o_ref.shape[0]
    slots = wide * PIECES
    extra = CORES * PIECES - KEPT
    far = line - 2
    left_end, right_end = g == 0, g == line - 1
    helps_left, helps_right = g == 1, g == far
    is_end = left_end | right_end
    helps = helps_left | helps_right
    partner = jnp.where(left_end | helps_right, w + CORES, w - CORES)
    chip_slots = CORES * PIECES
    lent = jnp.where(helps_left, slots - chip_slots, 0) + KEPT
    early = [i for i in range(extra) if (KEPT + i) % PIECES < PIECES - 1]
    missing = jnp.where(left_end, slots - chip_slots, 0) + KEPT

    def kept(slot):
        lacks = (left_end & (slot >= slots - chip_slots)) | (right_end & (slot < chip_slots))
        return ~(lacks & (slot % (CORES * PIECES) >= KEPT))

    load_a = pltpu.make_async_copy(a_hbm, a_ref, load_sem.at[0])
    load_b = pltpu.make_async_copy(b_hbm, b_ref, load_sem.at[1])
    load_b.start()
    load_a.start()
    barrier = pltpu.get_barrier_semaphore()

    def greet(wide_index, col_index):
        pl.semaphore_signal(barrier, inc=1, device_id={"wide": wide_index, "col": col_index}, device_id_type=MESH)

    has_left = g > 0
    has_right = g < line - 1
    pl.when(has_left)(lambda: greet(w - CORES, c))
    pl.when(has_right)(lambda: greet(w + CORES, c))
    greet(sibling, c)

    @pl.loop(1, cols)
    def _(j):
        greet(w, (c + j) % cols)

    pl.semaphore_wait(barrier, cols + has_left.astype(jnp.int32) + has_right.astype(jnp.int32))

    load_b.wait()

    def push(src, slot, sem, target):
        return pltpu.make_async_remote_copy(
            src_ref=src, dst_ref=panel.at[slot], send_sem=sem, recv_sem=recv_panel.at[slot],
            device_id={"wide": target, "col": c}, device_id_type=MESH)

    def own(h):
        return b_ref.at[pl.ds(h * rows, rows)]

    def arrive(slot):
        pltpu.make_async_copy(panel.at[slot], panel.at[slot], recv_panel.at[slot]).wait()

    def lend():
        return pltpu.make_async_remote_copy(
            src_ref=a_ref, dst_ref=guest, send_sem=send_guest, recv_sem=recv_guest,
            device_id={"wide": partner, "col": c}, device_id_type=MESH)

    def give_back(i):
        return pltpu.make_async_remote_copy(
            src_ref=outbox.at[i], dst_ref=inbox.at[i], send_sem=send_back.at[i], recv_sem=recv_back.at[i],
            device_id={"wide": partner, "col": c}, device_id_type=MESH)

    def contract(block, slot):
        contract_rows(a_high, a_low, block, slot)

    def contract_guest(slot, i):
        contract_rows(guest_high, guest_low, panel[slot], slots + i)

    def contract_rows(rows_high, rows_low, block, slot):
        high, low = halves(block)
        both = dot(rows_high[...], jnp.concatenate([high, low], axis=0))
        product = both[:, :rows] + (both[:, rows:] + dot(rows_low[...], high))
        for k in range(cols):
            part[slot, k] = product[k * share:(k + 1) * share]

        @pl.loop(1, cols)
        def _(j):
            peer = (c + j) % cols
            pltpu.make_async_remote_copy(
                src_ref=part.at[slot, peer], dst_ref=landed.at[slot, cols - 1 - j],
                send_sem=send_sum.at[slot], recv_sem=recv_sum.at[slot],
                device_id={"wide": w, "col": peer}, device_id_type=MESH).start()

    def summed(slot):
        pltpu.make_async_copy(landed.at[slot], landed.at[slot], recv_sum.at[slot]).wait()
        total = part[slot, c]
        for k in range(cols - 1):
            total = total + landed[slot, k]
        return total

    def place(slot, block):
        o_ref[:, pl.ds(pl.multiple_of(slot * rows, rows), rows)] = block

    for h in range(PIECES):
        slot = w * PIECES + h
        pl.when(has_right)(lambda: push(own(h), slot, send_line.at[slot], w + CORES).start())
        pl.when(has_left)(lambda: push(own(h), slot, send_line.at[wide * PIECES + h], w - CORES).start())
        push(own(h), slot, send_pair.at[slot], sibling).start()

    load_a.wait()
    high, low = halves(a_ref[...])
    a_high[...] = high
    a_low[...] = low
    for h in range(PIECES):
        contract(b_ref[h * rows:(h + 1) * rows], w * PIECES + h)
    for h in range(PIECES):
        slot = sibling * PIECES + h
        arrive(slot)
        contract(panel[slot], slot)

    @pl.loop(1, line)
    def _(d):
        @pl.loop(0, slots)
        def _(slot):
            away = slot // chip_slots - g
            pl.when((d >= 2) & (jnp.maximum(away, -away) == d - 2) & kept(slot) & (d - 2 < line - 2))(lambda: place(slot, summed(slot)))

        @pl.loop(0, PIECES)
        def _(h):
            left_slot = (w - d * CORES) * PIECES + h
            right_slot = (w + d * CORES) * PIECES + h
            pair_left = (sibling - d * CORES) * PIECES + h
            pair_right = (sibling + d * CORES) * PIECES + h

            @pl.when((g - d >= 0) & ((d <= far) | (core * PIECES + h < KEPT)))
            def _():
                arrive(left_slot)
                pl.when(has_right & ((d < far) | ((d == far) & (core * PIECES + h < KEPT))))(lambda: push(panel.at[left_slot], left_slot, send_line.at[left_slot], w + CORES).start())
                push(panel.at[left_slot], left_slot, send_pair.at[left_slot], sibling).start()

            @pl.when((g + d < line) & ((d <= far) | (core * PIECES + h < KEPT)))
            def _():
                arrive(right_slot)
                pl.when(has_left & ((d < far) | ((d == far) & (core * PIECES + h < KEPT))))(lambda: push(panel.at[right_slot], right_slot, send_line.at[right_slot], w - CORES).start())
                push(panel.at[right_slot], right_slot, send_pair.at[right_slot], sibling).start()

            pl.when(is_end & (d == 1) & (h == PIECES - 1))(lambda: lend().start())
            last = (d == far) & (h == PIECES - 1)

            @pl.when(helps & last)
            def _():
                pltpu.make_async_copy(guest, guest, recv_guest).wait()
                high, low = halves(guest[...])
                guest_high[...] = high
                guest_low[...] = low
                for i in early:
                    contract_guest(lent + i, i)

                def late(k):
                    i = k * PIECES + PIECES - 1 - KEPT
                    pl.when(i >= 0)(lambda: contract_guest(lent + i, i))

                late(core)
                arrive(jnp.where(helps_left, pair_right, pair_left))
                late(1 - core)

            @pl.when((g - d >= 0) & ((d <= far) | (core * PIECES + h < KEPT)))
            def _():
                contract(panel[left_slot], left_slot)

            @pl.when((g + d < line) & ((d <= far) | (core * PIECES + h < KEPT)))
            def _():
                contract(panel[right_slot], right_slot)

            @pl.when((g - d >= 0) & ((d <= far) | ((1 - core) * PIECES + h < KEPT)))
            def _():
                pl.when(~(helps_right & last))(lambda: arrive(pair_left))
                contract(panel[pair_left], pair_left)

            @pl.when((g + d < line) & ((d <= far) | ((1 - core) * PIECES + h < KEPT)))
            def _():
                pl.when(~(helps_left & last))(lambda: arrive(pair_right))
                contract(panel[pair_right], pair_right)

    @pl.when(helps)
    def _():
        for i in early + [i for i in range(extra) if i not in early]:
            outbox[i] = summed(slots + i)
            give_back(i).start()

    @pl.loop(0, slots)
    def _(slot):
        away = slot // chip_slots - g
        pl.when(kept(slot) & (jnp.maximum(away, -away) >= line - 2))(lambda: place(slot, summed(slot)))

    @pl.when(is_end)
    def _():
        @pl.loop(0, extra)
        def _(i):
            pltpu.make_async_copy(inbox.at[i], inbox.at[i], recv_back.at[i]).wait()
            place(missing + i, inbox[i])

    for h in range(PIECES):
        slot = w * PIECES + h
        pl.when(has_right)(lambda: push(own(h), slot, send_line.at[slot], w + CORES).wait_send())
        pl.when(has_left)(lambda: push(own(h), slot, send_line.at[wide * PIECES + h], w - CORES).wait_send())
        push(own(h), slot, send_pair.at[slot], sibling).wait_send()

    @pl.loop(1, line)
    def _(d):
        @pl.loop(0, PIECES)
        def _(h):
            left_slot = (w - d * CORES) * PIECES + h
            right_slot = (w + d * CORES) * PIECES + h

            @pl.when((g - d >= 0) & ((d <= far) | (core * PIECES + h < KEPT)))
            def _():
                pl.when(has_right & ((d < far) | ((d == far) & (core * PIECES + h < KEPT))))(lambda: push(panel.at[left_slot], left_slot, send_line.at[left_slot], w + CORES).wait_send())
                push(panel.at[left_slot], left_slot, send_pair.at[left_slot], sibling).wait_send()

            @pl.when((g + d < line) & ((d <= far) | (core * PIECES + h < KEPT)))
            def _():
                pl.when(has_left & ((d < far) | ((d == far) & (core * PIECES + h < KEPT))))(lambda: push(panel.at[right_slot], right_slot, send_line.at[right_slot], w - CORES).wait_send())
                push(panel.at[right_slot], right_slot, send_pair.at[right_slot], sibling).wait_send()

    def sent(slot):
        pltpu.make_async_copy(landed.at[slot], landed.at[slot], send_sum.at[slot]).wait()

    @pl.loop(0, slots)
    def _(slot):
        pl.when(kept(slot))(lambda: sent(slot))

    @pl.when(helps)
    def _():
        @pl.loop(0, extra)
        def _(i):
            sent(slots + i)
            give_back(i).wait_send()

    pl.when(is_end)(lambda: lend().wait_send())


def on_device(wide, cols, amplitudes, integrals):
    rows_a, depth = amplitudes.shape
    rows_b = integrals.shape[0]
    share = rows_a // cols
    slots = wide * PIECES
    extra = CORES * PIECES - KEPT
    rows = rows_b // PIECES
    vmem = pl.BlockSpec(memory_space=pltpu.VMEM)
    padded = -(-share // 8) * 8
    held = 4 * (4 * rows_a * depth + (slots + PIECES) * rows * depth + (slots + extra) * 2 * cols * padded * rows)
    limit = held + 12 * 1024 * 1024
    return pl.pallas_call(
        functools.partial(kernel, wide, cols),
        out_shape=jax.ShapeDtypeStruct((share, wide * rows_b), jnp.float32),
        in_specs=[pl.BlockSpec(memory_space=pltpu.HBM)] * 2,
        out_specs=vmem,
        scratch_shapes=[
            pltpu.VMEM((rows_a, depth), jnp.float32),
            pltpu.VMEM((rows_b, depth), jnp.float32),
            pltpu.SemaphoreType.DMA((2,)),
            pltpu.VMEM((slots, rows, depth), jnp.float32),
            pltpu.VMEM((rows_a, depth), jnp.bfloat16),
            pltpu.VMEM((rows_a, depth), jnp.bfloat16),
            pltpu.VMEM((slots + extra, cols, share, rows), jnp.float32),
            pltpu.VMEM((slots + extra, cols - 1, share, rows), jnp.float32),
            pltpu.VMEM((rows_a, depth), jnp.float32),
            pltpu.VMEM((rows_a, depth), jnp.bfloat16),
            pltpu.VMEM((rows_a, depth), jnp.bfloat16),
            pltpu.VMEM((extra, share, rows), jnp.float32),
            pltpu.VMEM((extra, share, rows), jnp.float32),
            pltpu.SemaphoreType.DMA((slots + PIECES,)),
            pltpu.SemaphoreType.DMA((slots,)),
            pltpu.SemaphoreType.DMA((slots,)),
            pltpu.SemaphoreType.DMA((slots + extra,)),
            pltpu.SemaphoreType.DMA((slots + extra,)),
            pltpu.SemaphoreType.DMA,
            pltpu.SemaphoreType.DMA,
            pltpu.SemaphoreType.DMA((extra,)),
            pltpu.SemaphoreType.DMA((extra,)),
        ],
        compiler_params=pltpu.CompilerParams(
            collective_id=0, has_side_effects=True, vmem_limit_bytes=limit),
    )(pltpu.with_memory_space_constraint(amplitudes, pltpu.HBM), pltpu.with_memory_space_constraint(integrals, pltpu.HBM))


def solution(mesh):
    return jax.shard_map(
        functools.partial(on_device, mesh.shape["wide"], mesh.shape["col"]),
        mesh=mesh,
        in_specs=(P("wide", "col"), P("wide", "col")),
        out_specs=P(("wide", "col"), None),
        check_vma=False,
    )
```

```python
import functools

import jax
import jax.numpy as jnp
from jax import lax
from jax.experimental import pallas as pl
from jax.experimental.pallas import tpu as pltpu
from jax.sharding import PartitionSpec as P

MESH = pl.DeviceIdType.MESH
CORES = 2
PIECES = 2
KEPT = 1


def halves(x):
    high = x.astype(jnp.bfloat16)
    low = (x - high.astype(jnp.float32)).astype(jnp.bfloat16)
    return high, low


def dot(x, y):
    return lax.dot_general(x, y, (((1,), (1,)), ((), ())), preferred_element_type=jnp.float32)


def kernel(wide, cols, a_hbm, b_hbm, o_ref, a_ref, b_ref, load_sem, panel, a_high, a_low, part, landed,
           guest, guest_high, guest_low, outbox, inbox,
           send_line, send_pair, recv_panel, send_sum, recv_sum,
           send_guest, recv_guest, send_back, recv_back):
    w = lax.axis_index("wide")
    c = lax.axis_index("col")
    line = wide // CORES
    g = w // CORES
    core = w % CORES
    sibling = g * CORES + 1 - core
    rows = b_ref.shape[0] // PIECES
    share = o_ref.shape[0]
    slots = wide * PIECES
    extra = CORES * PIECES - KEPT
    far = line - 2
    left_end, right_end = g == 0, g == line - 1
    helps_left, helps_right = g == 1, g == far
    is_end = left_end | right_end
    helps = helps_left | helps_right
    partner = jnp.where(left_end | helps_right, w + CORES, w - CORES)
    chip_slots = CORES * PIECES
    lent = jnp.where(helps_left, slots - chip_slots, 0) + KEPT
    early = [i for i in range(extra) if (KEPT + i) % PIECES < PIECES - 1]
    missing = jnp.where(left_end, slots - chip_slots, 0) + KEPT

    def kept(slot):
        lacks = (left_end & (slot >= slots - chip_slots)) | (right_end & (slot < chip_slots))
        return ~(lacks & (slot % (CORES * PIECES) >= KEPT))

    load_a = pltpu.make_async_copy(a_hbm, a_ref, load_sem.at[0])
    load_b = pltpu.make_async_copy(b_hbm, b_ref, load_sem.at[1])
    load_b.start()
    load_a.start()
    barrier = pltpu.get_barrier_semaphore()

    def greet(wide_index, col_index):
        pl.semaphore_signal(barrier, inc=1, device_id={"wide": wide_index, "col": col_index}, device_id_type=MESH)

    has_left = g > 0
    has_right = g < line - 1
    pl.when(has_left)(lambda: greet(w - CORES, c))
    pl.when(has_right)(lambda: greet(w + CORES, c))
    greet(sibling, c)

    @pl.loop(1, cols)
    def _(j):
        greet(w, (c + j) % cols)

    pl.semaphore_wait(barrier, cols + has_left.astype(jnp.int32) + has_right.astype(jnp.int32))

    load_b.wait()

    def push(src, slot, sem, target):
        return pltpu.make_async_remote_copy(
            src_ref=src, dst_ref=panel.at[slot], send_sem=sem, recv_sem=recv_panel.at[slot],
            device_id={"wide": target, "col": c}, device_id_type=MESH)

    def own(h):
        return b_ref.at[pl.ds(h * rows, rows)]

    def arrive(slot):
        pltpu.make_async_copy(panel.at[slot], panel.at[slot], recv_panel.at[slot]).wait()

    def lend():
        return pltpu.make_async_remote_copy(
            src_ref=a_ref, dst_ref=guest, send_sem=send_guest, recv_sem=recv_guest,
            device_id={"wide": partner, "col": c}, device_id_type=MESH)

    def give_back(i):
        return pltpu.make_async_remote_copy(
            src_ref=outbox.at[i], dst_ref=inbox.at[i], send_sem=send_back.at[i], recv_sem=recv_back.at[i],
            device_id={"wide": partner, "col": c}, device_id_type=MESH)

    def contract(block, slot):
        contract_rows(a_high, a_low, block, slot)

    def contract_guest(slot, i):
        contract_rows(guest_high, guest_low, panel[slot], slots + i)

    def contract_rows(rows_high, rows_low, block, slot):
        high, low = halves(block)
        both = dot(rows_high[...], jnp.concatenate([high, low], axis=0))
        product = both[:, :rows] + (both[:, rows:] + dot(rows_low[...], high))
        for k in range(cols):
            part[slot, k] = product[k * share:(k + 1) * share]

        @pl.loop(1, cols)
        def _(j):
            peer = (c + j) % cols
            pltpu.make_async_remote_copy(
                src_ref=part.at[slot, peer], dst_ref=landed.at[slot, cols - 1 - j],
                send_sem=send_sum.at[slot], recv_sem=recv_sum.at[slot],
                device_id={"wide": w, "col": peer}, device_id_type=MESH).start()

    def summed(slot):
        pltpu.make_async_copy(landed.at[slot], landed.at[slot], recv_sum.at[slot]).wait()
        total = part[slot, c]
        for k in range(cols - 1):
            total = total + landed[slot, k]
        return total

    def place(slot, block):
        o_ref[:, pl.ds(pl.multiple_of(slot * rows, rows), rows)] = block

    for h in range(PIECES):
        slot = w * PIECES + h
        pl.when(has_right)(lambda: push(own(h), slot, send_line.at[slot], w + CORES).start())
        pl.when(has_left)(lambda: push(own(h), slot, send_line.at[wide * PIECES + h], w - CORES).start())
        push(own(h), slot, send_pair.at[slot], sibling).start()

    load_a.wait()
    pl.when(is_end)(lambda: lend().start())
    high, low = halves(a_ref[...])
    a_high[...] = high
    a_low[...] = low
    for h in range(PIECES):
        contract(b_ref[h * rows:(h + 1) * rows], w * PIECES + h)
    for h in range(PIECES):
        slot = sibling * PIECES + h
        arrive(slot)
        contract(panel[slot], slot)

    @pl.loop(1, line)
    def _(d):
        @pl.loop(0, slots)
        def _(slot):
            away = slot // chip_slots - g
            pl.when((d >= 2) & (jnp.maximum(away, -away) == d - 2) & kept(slot) & (d - 2 < line - 2))(lambda: place(slot, summed(slot)))

        @pl.loop(0, PIECES)
        def _(h):
            left_slot = (w - d * CORES) * PIECES + h
            right_slot = (w + d * CORES) * PIECES + h
            pair_left = (sibling - d * CORES) * PIECES + h
            pair_right = (sibling + d * CORES) * PIECES + h

            @pl.when((g - d >= 0) & ((d <= far) | (core * PIECES + h < KEPT)))
            def _():
                arrive(left_slot)
                pl.when(has_right & ((d < far) | ((d == far) & (core * PIECES + h < KEPT))))(lambda: push(panel.at[left_slot], left_slot, send_line.at[left_slot], w + CORES).start())
                push(panel.at[left_slot], left_slot, send_pair.at[left_slot], sibling).start()

            @pl.when((g + d < line) & ((d <= far) | (core * PIECES + h < KEPT)))
            def _():
                arrive(right_slot)
                pl.when(has_left & ((d < far) | ((d == far) & (core * PIECES + h < KEPT))))(lambda: push(panel.at[right_slot], right_slot, send_line.at[right_slot], w - CORES).start())
                push(panel.at[right_slot], right_slot, send_pair.at[right_slot], sibling).start()

            last = (d == far) & (h == PIECES - 1)

            @pl.when(helps & last)
            def _():
                pltpu.make_async_copy(guest, guest, recv_guest).wait()
                high, low = halves(guest[...])
                guest_high[...] = high
                guest_low[...] = low
                for i in early:
                    contract_guest(lent + i, i)

                def late(k):
                    i = k * PIECES + PIECES - 1 - KEPT
                    pl.when(i >= 0)(lambda: contract_guest(lent + i, i))

                late(core)
                arrive(jnp.where(helps_left, pair_right, pair_left))
                late(1 - core)

            @pl.when((g - d >= 0) & ((d <= far) | (core * PIECES + h < KEPT)))
            def _():
                contract(panel[left_slot], left_slot)

            @pl.when((g + d < line) & ((d <= far) | (core * PIECES + h < KEPT)))
            def _():
                contract(panel[right_slot], right_slot)

            @pl.when((g - d >= 0) & ((d <= far) | ((1 - core) * PIECES + h < KEPT)))
            def _():
                pl.when(~(helps_right & last))(lambda: arrive(pair_left))
                contract(panel[pair_left], pair_left)

            @pl.when((g + d < line) & ((d <= far) | ((1 - core) * PIECES + h < KEPT)))
            def _():
                pl.when(~(helps_left & last))(lambda: arrive(pair_right))
                contract(panel[pair_right], pair_right)

    @pl.when(helps)
    def _():
        for i in early + [i for i in range(extra) if i not in early]:
            outbox[i] = summed(slots + i)
            give_back(i).start()

    @pl.loop(0, slots)
    def _(slot):
        away = slot // chip_slots - g
        pl.when(kept(slot) & (jnp.maximum(away, -away) >= line - 2))(lambda: place(slot, summed(slot)))

    @pl.when(is_end)
    def _():
        @pl.loop(0, extra)
        def _(i):
            pltpu.make_async_copy(inbox.at[i], inbox.at[i], recv_back.at[i]).wait()
            place(missing + i, inbox[i])

    for h in range(PIECES):
        slot = w * PIECES + h
        pl.when(has_right)(lambda: push(own(h), slot, send_line.at[slot], w + CORES).wait_send())
        pl.when(has_left)(lambda: push(own(h), slot, send_line.at[wide * PIECES + h], w - CORES).wait_send())
        push(own(h), slot, send_pair.at[slot], sibling).wait_send()

    @pl.loop(1, line)
    def _(d):
        @pl.loop(0, PIECES)
        def _(h):
            left_slot = (w - d * CORES) * PIECES + h
            right_slot = (w + d * CORES) * PIECES + h

            @pl.when((g - d >= 0) & ((d <= far) | (core * PIECES + h < KEPT)))
            def _():
                pl.when(has_right & ((d < far) | ((d == far) & (core * PIECES + h < KEPT))))(lambda: push(panel.at[left_slot], left_slot, send_line.at[left_slot], w + CORES).wait_send())
                push(panel.at[left_slot], left_slot, send_pair.at[left_slot], sibling).wait_send()

            @pl.when((g + d < line) & ((d <= far) | (core * PIECES + h < KEPT)))
            def _():
                pl.when(has_left & ((d < far) | ((d == far) & (core * PIECES + h < KEPT))))(lambda: push(panel.at[right_slot], right_slot, send_line.at[right_slot], w - CORES).wait_send())
                push(panel.at[right_slot], right_slot, send_pair.at[right_slot], sibling).wait_send()

    def sent(slot):
        pltpu.make_async_copy(landed.at[slot], landed.at[slot], send_sum.at[slot]).wait()

    @pl.loop(0, slots)
    def _(slot):
        pl.when(kept(slot))(lambda: sent(slot))

    @pl.when(helps)
    def _():
        @pl.loop(0, extra)
        def _(i):
            sent(slots + i)
            give_back(i).wait_send()

    pl.when(is_end)(lambda: lend().wait_send())


def on_device(wide, cols, amplitudes, integrals):
    rows_a, depth = amplitudes.shape
    rows_b = integrals.shape[0]
    share = rows_a // cols
    slots = wide * PIECES
    extra = CORES * PIECES - KEPT
    rows = rows_b // PIECES
    vmem = pl.BlockSpec(memory_space=pltpu.VMEM)
    padded = -(-share // 8) * 8
    held = 4 * (4 * rows_a * depth + (slots + PIECES) * rows * depth + (slots + extra) * 2 * cols * padded * rows)
    limit = held + 12 * 1024 * 1024
    return pl.pallas_call(
        functools.partial(kernel, wide, cols),
        out_shape=jax.ShapeDtypeStruct((share, wide * rows_b), jnp.float32),
        in_specs=[pl.BlockSpec(memory_space=pltpu.HBM)] * 2,
        out_specs=vmem,
        scratch_shapes=[
            pltpu.VMEM((rows_a, depth), jnp.float32),
            pltpu.VMEM((rows_b, depth), jnp.float32),
            pltpu.SemaphoreType.DMA((2,)),
            pltpu.VMEM((slots, rows, depth), jnp.float32),
            pltpu.VMEM((rows_a, depth), jnp.bfloat16),
            pltpu.VMEM((rows_a, depth), jnp.bfloat16),
            pltpu.VMEM((slots + extra, cols, share, rows), jnp.float32),
            pltpu.VMEM((slots + extra, cols - 1, share, rows), jnp.float32),
            pltpu.VMEM((rows_a, depth), jnp.float32),
            pltpu.VMEM((rows_a, depth), jnp.bfloat16),
            pltpu.VMEM((rows_a, depth), jnp.bfloat16),
            pltpu.VMEM((extra, share, rows), jnp.float32),
            pltpu.VMEM((extra, share, rows), jnp.float32),
            pltpu.SemaphoreType.DMA((slots + PIECES,)),
            pltpu.SemaphoreType.DMA((slots,)),
            pltpu.SemaphoreType.DMA((slots,)),
            pltpu.SemaphoreType.DMA((slots + extra,)),
            pltpu.SemaphoreType.DMA((slots + extra,)),
            pltpu.SemaphoreType.DMA,
            pltpu.SemaphoreType.DMA,
            pltpu.SemaphoreType.DMA((extra,)),
            pltpu.SemaphoreType.DMA((extra,)),
        ],
        compiler_params=pltpu.CompilerParams(
            collective_id=0, has_side_effects=True, vmem_limit_bytes=limit),
    )(pltpu.with_memory_space_constraint(amplitudes, pltpu.HBM), pltpu.with_memory_space_constraint(integrals, pltpu.HBM))


def solution(mesh):
    return jax.shard_map(
        functools.partial(on_device, mesh.shape["wide"], mesh.shape["col"]),
        mesh=mesh,
        in_specs=(P("wide", "col"), P("wide", "col")),
        out_specs=P(("wide", "col"), None),
        check_vma=False,
    )
```

```python
import functools

import jax
import jax.numpy as jnp
from jax import lax
from jax.experimental import pallas as pl
from jax.experimental.pallas import tpu as pltpu
from jax.sharding import PartitionSpec as P

MESH = pl.DeviceIdType.MESH
CORES = 2
PIECES = 2
KEPT = 1


def halves(x):
    high = x.astype(jnp.bfloat16)
    low = (x - high.astype(jnp.float32)).astype(jnp.bfloat16)
    return high, low


def dot(x, y):
    return lax.dot_general(x, y, (((1,), (1,)), ((), ())), preferred_element_type=jnp.float32)


def kernel(wide, cols, a_hbm, b_hbm, o_ref, a_ref, b_ref, load_sem, panel, a_high, a_low, part, landed,
           guest, guest_high, guest_low, outbox, inbox,
           send_line, send_pair, recv_panel, send_sum, recv_sum,
           send_guest, recv_guest, send_back, recv_back):
    w = lax.axis_index("wide")
    c = lax.axis_index("col")
    line = wide // CORES
    g = w // CORES
    core = w % CORES
    sibling = g * CORES + 1 - core
    rows = b_ref.shape[0] // PIECES
    share = o_ref.shape[0]
    half = guest.shape[0] // CORES
    slots = wide * PIECES
    extra = CORES * PIECES - KEPT
    far = line - 2
    left_end, right_end = g == 0, g == line - 1
    helps_left, helps_right = g == 1, g == far
    is_end = left_end | right_end
    helps = helps_left | helps_right
    partner = jnp.where(left_end | helps_right, w + CORES, w - CORES)
    chip_slots = CORES * PIECES
    lent = jnp.where(helps_left, slots - chip_slots, 0) + KEPT
    early = [i for i in range(extra) if (KEPT + i) % PIECES < PIECES - 1]
    missing = jnp.where(left_end, slots - chip_slots, 0) + KEPT

    def kept(slot):
        lacks = (left_end & (slot >= slots - chip_slots)) | (right_end & (slot < chip_slots))
        return ~(lacks & (slot % (CORES * PIECES) >= KEPT))

    load_a = pltpu.make_async_copy(a_hbm, a_ref, load_sem.at[0])
    load_b = pltpu.make_async_copy(b_hbm, b_ref, load_sem.at[1])
    load_b.start()
    load_a.start()
    barrier = pltpu.get_barrier_semaphore()

    def greet(wide_index, col_index):
        pl.semaphore_signal(barrier, inc=1, device_id={"wide": wide_index, "col": col_index}, device_id_type=MESH)

    has_left = g > 0
    has_right = g < line - 1
    pl.when(has_left)(lambda: greet(w - CORES, c))
    pl.when(has_right)(lambda: greet(w + CORES, c))
    greet(sibling, c)

    @pl.loop(1, cols)
    def _(j):
        greet(w, (c + j) % cols)

    pl.semaphore_wait(barrier, cols + has_left.astype(jnp.int32) + has_right.astype(jnp.int32))

    load_b.wait()

    def push(src, slot, sem, target):
        return pltpu.make_async_remote_copy(
            src_ref=src, dst_ref=panel.at[slot], send_sem=sem, recv_sem=recv_panel.at[slot],
            device_id={"wide": target, "col": c}, device_id_type=MESH)

    def own(h):
        return b_ref.at[pl.ds(h * rows, rows)]

    def arrive(slot):
        pltpu.make_async_copy(panel.at[slot], panel.at[slot], recv_panel.at[slot]).wait()

    def lend(i):
        return pltpu.make_async_remote_copy(
            src_ref=a_ref.at[pl.ds(i * half, half)], dst_ref=guest.at[pl.ds(i * half, half)], send_sem=send_guest.at[i], recv_sem=recv_guest.at[i],
            device_id={"wide": partner, "col": c}, device_id_type=MESH)

    def give_back(i):
        return pltpu.make_async_remote_copy(
            src_ref=outbox.at[i], dst_ref=inbox.at[i], send_sem=send_back.at[i], recv_sem=recv_back.at[i],
            device_id={"wide": partner, "col": c}, device_id_type=MESH)

    def contract(block, slot):
        contract_rows(a_high, a_low, block, slot)

    def contract_guest(slot, i):
        contract_rows(guest_high, guest_low, panel[slot], slots + i)

    def contract_rows(rows_high, rows_low, block, slot):
        high, low = halves(block)
        both = dot(rows_high[...], jnp.concatenate([high, low], axis=0))
        product = both[:, :rows] + (both[:, rows:] + dot(rows_low[...], high))
        for k in range(cols):
            part[slot, k] = product[k * share:(k + 1) * share]

        @pl.loop(1, cols)
        def _(j):
            peer = (c + j) % cols
            pltpu.make_async_remote_copy(
                src_ref=part.at[slot, peer], dst_ref=landed.at[slot, cols - 1 - j],
                send_sem=send_sum.at[slot], recv_sem=recv_sum.at[slot],
                device_id={"wide": w, "col": peer}, device_id_type=MESH).start()

    def summed(slot):
        pltpu.make_async_copy(landed.at[slot], landed.at[slot], recv_sum.at[slot]).wait()
        total = part[slot, c]
        for k in range(cols - 1):
            total = total + landed[slot, k]
        return total

    def place(slot, block):
        o_ref[:, pl.ds(pl.multiple_of(slot * rows, rows), rows)] = block

    for h in range(PIECES):
        slot = w * PIECES + h
        pl.when(has_right)(lambda: push(own(h), slot, send_line.at[slot], w + CORES).start())
        pl.when(has_left)(lambda: push(own(h), slot, send_line.at[wide * PIECES + h], w - CORES).start())
        push(own(h), slot, send_pair.at[slot], sibling).start()

    load_a.wait()
    for i in range(CORES):
        pl.when(is_end)(lambda: lend(i).start())
    high, low = halves(a_ref[...])
    a_high[...] = high
    a_low[...] = low
    for h in range(PIECES):
        contract(b_ref[h * rows:(h + 1) * rows], w * PIECES + h)
    for h in range(PIECES):
        slot = sibling * PIECES + h
        arrive(slot)
        contract(panel[slot], slot)

    @pl.loop(1, line)
    def _(d):
        @pl.loop(0, slots)
        def _(slot):
            away = slot // chip_slots - g
            pl.when((d >= 2) & (jnp.maximum(away, -away) == d - 2) & kept(slot) & (d - 2 < line - 2))(lambda: place(slot, summed(slot)))

        @pl.loop(0, PIECES)
        def _(h):
            left_slot = (w - d * CORES) * PIECES + h
            right_slot = (w + d * CORES) * PIECES + h
            pair_left = (sibling - d * CORES) * PIECES + h
            pair_right = (sibling + d * CORES) * PIECES + h

            @pl.when((g - d >= 0) & ((d <= far) | (core * PIECES + h < KEPT)))
            def _():
                arrive(left_slot)
                pl.when(has_right & ((d < far) | ((d == far) & (core * PIECES + h < KEPT))))(lambda: push(panel.at[left_slot], left_slot, send_line.at[left_slot], w + CORES).start())
                push(panel.at[left_slot], left_slot, send_pair.at[left_slot], sibling).start()

            @pl.when((g + d < line) & ((d <= far) | (core * PIECES + h < KEPT)))
            def _():
                arrive(right_slot)
                pl.when(has_left & ((d < far) | ((d == far) & (core * PIECES + h < KEPT))))(lambda: push(panel.at[right_slot], right_slot, send_line.at[right_slot], w - CORES).start())
                push(panel.at[right_slot], right_slot, send_pair.at[right_slot], sibling).start()

            last = (d == far) & (h == PIECES - 1)

            @pl.when(helps & last)
            def _():
                for i in range(CORES):
                    lines = guest.at[pl.ds(i * half, half)]
                    pltpu.make_async_copy(lines, lines, recv_guest.at[i]).wait()
                    high, low = halves(lines[...])
                    guest_high[i * half:(i + 1) * half] = high
                    guest_low[i * half:(i + 1) * half] = low
                for i in early:
                    contract_guest(lent + i, i)

                def late(k):
                    i = k * PIECES + PIECES - 1 - KEPT
                    pl.when(i >= 0)(lambda: contract_guest(lent + i, i))

                late(core)
                arrive(jnp.where(helps_left, pair_right, pair_left))
                late(1 - core)

            @pl.when((g - d >= 0) & ((d <= far) | (core * PIECES + h < KEPT)))
            def _():
                contract(panel[left_slot], left_slot)

            @pl.when((g + d < line) & ((d <= far) | (core * PIECES + h < KEPT)))
            def _():
                contract(panel[right_slot], right_slot)

            @pl.when((g - d >= 0) & ((d <= far) | ((1 - core) * PIECES + h < KEPT)))
            def _():
                pl.when(~(helps_right & last))(lambda: arrive(pair_left))
                contract(panel[pair_left], pair_left)

            @pl.when((g + d < line) & ((d <= far) | ((1 - core) * PIECES + h < KEPT)))
            def _():
                pl.when(~(helps_left & last))(lambda: arrive(pair_right))
                contract(panel[pair_right], pair_right)

    @pl.when(helps)
    def _():
        for i in early + [i for i in range(extra) if i not in early]:
            outbox[i] = summed(slots + i)
            give_back(i).start()

    @pl.loop(0, slots)
    def _(slot):
        away = slot // chip_slots - g
        pl.when(kept(slot) & (jnp.maximum(away, -away) >= line - 2))(lambda: place(slot, summed(slot)))

    @pl.when(is_end)
    def _():
        @pl.loop(0, extra)
        def _(i):
            pltpu.make_async_copy(inbox.at[i], inbox.at[i], recv_back.at[i]).wait()
            place(missing + i, inbox[i])

    for h in range(PIECES):
        slot = w * PIECES + h
        pl.when(has_right)(lambda: push(own(h), slot, send_line.at[slot], w + CORES).wait_send())
        pl.when(has_left)(lambda: push(own(h), slot, send_line.at[wide * PIECES + h], w - CORES).wait_send())
        push(own(h), slot, send_pair.at[slot], sibling).wait_send()

    @pl.loop(1, line)
    def _(d):
        @pl.loop(0, PIECES)
        def _(h):
            left_slot = (w - d * CORES) * PIECES + h
            right_slot = (w + d * CORES) * PIECES + h

            @pl.when((g - d >= 0) & ((d <= far) | (core * PIECES + h < KEPT)))
            def _():
                pl.when(has_right & ((d < far) | ((d == far) & (core * PIECES + h < KEPT))))(lambda: push(panel.at[left_slot], left_slot, send_line.at[left_slot], w + CORES).wait_send())
                push(panel.at[left_slot], left_slot, send_pair.at[left_slot], sibling).wait_send()

            @pl.when((g + d < line) & ((d <= far) | (core * PIECES + h < KEPT)))
            def _():
                pl.when(has_left & ((d < far) | ((d == far) & (core * PIECES + h < KEPT))))(lambda: push(panel.at[right_slot], right_slot, send_line.at[right_slot], w - CORES).wait_send())
                push(panel.at[right_slot], right_slot, send_pair.at[right_slot], sibling).wait_send()

    def sent(slot):
        pltpu.make_async_copy(landed.at[slot], landed.at[slot], send_sum.at[slot]).wait()

    @pl.loop(0, slots)
    def _(slot):
        pl.when(kept(slot))(lambda: sent(slot))

    @pl.when(helps)
    def _():
        @pl.loop(0, extra)
        def _(i):
            sent(slots + i)
            give_back(i).wait_send()

    for i in range(CORES):
        pl.when(is_end)(lambda: lend(i).wait_send())


def on_device(wide, cols, amplitudes, integrals):
    rows_a, depth = amplitudes.shape
    rows_b = integrals.shape[0]
    share = rows_a // cols
    slots = wide * PIECES
    extra = CORES * PIECES - KEPT
    rows = rows_b // PIECES
    vmem = pl.BlockSpec(memory_space=pltpu.VMEM)
    padded = -(-share // 8) * 8
    held = 4 * (4 * rows_a * depth + (slots + PIECES) * rows * depth + (slots + extra) * 2 * cols * padded * rows)
    limit = held + 12 * 1024 * 1024
    return pl.pallas_call(
        functools.partial(kernel, wide, cols),
        out_shape=jax.ShapeDtypeStruct((share, wide * rows_b), jnp.float32),
        in_specs=[pl.BlockSpec(memory_space=pltpu.HBM)] * 2,
        out_specs=vmem,
        scratch_shapes=[
            pltpu.VMEM((rows_a, depth), jnp.float32),
            pltpu.VMEM((rows_b, depth), jnp.float32),
            pltpu.SemaphoreType.DMA((2,)),
            pltpu.VMEM((slots, rows, depth), jnp.float32),
            pltpu.VMEM((rows_a, depth), jnp.bfloat16),
            pltpu.VMEM((rows_a, depth), jnp.bfloat16),
            pltpu.VMEM((slots + extra, cols, share, rows), jnp.float32),
            pltpu.VMEM((slots + extra, cols - 1, share, rows), jnp.float32),
            pltpu.VMEM((rows_a, depth), jnp.float32),
            pltpu.VMEM((rows_a, depth), jnp.bfloat16),
            pltpu.VMEM((rows_a, depth), jnp.bfloat16),
            pltpu.VMEM((extra, share, rows), jnp.float32),
            pltpu.VMEM((extra, share, rows), jnp.float32),
            pltpu.SemaphoreType.DMA((slots + PIECES,)),
            pltpu.SemaphoreType.DMA((slots,)),
            pltpu.SemaphoreType.DMA((slots,)),
            pltpu.SemaphoreType.DMA((slots + extra,)),
            pltpu.SemaphoreType.DMA((slots + extra,)),
            pltpu.SemaphoreType.DMA((CORES,)),
            pltpu.SemaphoreType.DMA((CORES,)),
            pltpu.SemaphoreType.DMA((extra,)),
            pltpu.SemaphoreType.DMA((extra,)),
        ],
        compiler_params=pltpu.CompilerParams(
            collective_id=0, has_side_effects=True, vmem_limit_bytes=limit),
    )(pltpu.with_memory_space_constraint(amplitudes, pltpu.HBM), pltpu.with_memory_space_constraint(integrals, pltpu.HBM))


def solution(mesh):
    return jax.shard_map(
        functools.partial(on_device, mesh.shape["wide"], mesh.shape["col"]),
        mesh=mesh,
        in_specs=(P("wide", "col"), P("wide", "col")),
        out_specs=P(("wide", "col"), None),
        check_vma=False,
    )
```
